32 devices in a mesh: lat: 4 (over z), lon: 8 (over y, x, core).
Axes of the slice: x: 2, y: 2, z: 4, core: 2. Of those that a mesh axis runs over, the one named last changes fastest.
Arguments:
- tracers: float32 [16, 8, 64, 1024], P(None, None, 'lat', 'lon'), may hold values from -6 to 6
- winds: float32 [3, 8, 64, 1024], P(None, None, 'lat', 'lon'), may hold values from -4 to 4
- depart_first: int32 [3, 8, 64, 1024], P(None, None, 'lat', 'lon'), may hold values from -3 to 2, as said below
- depart_second: int32 [3, 8, 64, 1024], P(None, None, 'lat', 'lon'), may hold values from -2 to 1, as said below
- fluxes: bfloat16 [384, 128, 256], P(('lat', 'lon')), may hold values from 0.049804688 to 5
- remap_weights: bfloat16 [384, 4, 256, 128], P(('lat', 'lon')), may hold values from 0.00019931793 to 0.019897461
- target_device: int32 [384, 4], P(('lat', 'lon')), may hold values from 0 to 31, all different within a row; in each aligned block of 12 rows (0 to 11, 12 to 23, ...) at most 2 rows name the same one
- target_block: int32 [384, 4], P(('lat', 'lon')), may hold values from 0 to 15
Outputs:
- advected: float32 [16, 8, 64, 1024], P(None, None, 'lat', 'lon')
The draws below stay inside these ranges and needn't reach their ends.
Inputs may be any that keep to these rules, and one draw needn't show every extreme that they name: `depart_first`: component 0 (levels) is -1 or 0; components 1 and 2 are row and column offsets. `depart_second`: component 0 (levels) is -1 or 0; components 1 and 2 are row and column offsets. `target_device`: device g is the one at lat index g // 8 and lon index g % 8. Each row names 4 different devices; among the rows of one device no device is named more than 2 times.
All inputs are finite; a program needn't handle non-finite values.
Results may differ from the reference program's by a relative error of at most 0.00088.
Values may be sent and summed in bfloat16 or wider, within the bound.
A program may use at most 192 MiB of HBM per device.

```python
import math
import jax
import jax.numpy as jnp
import numpy as np
from jax import lax

NTR = 16
LEV = 8
CLAT = 16
CLON = 128
K = 4
CAP = 2
NTILE = 12
TILE_CELLS = 256
BLK_DEV = 16
HMAX = 3
ROWS = 128
BCOLS = 128
NLAT = 64
NLON = 1024
TILES = 384
N_LAT = 4
N_LON = 8
DEVICES = 32


def offsets_first(key):
    vertical = jax.random.randint(jax.random.fold_in(key, 1), (1, LEV, NLAT, NLON), -1, 1)
    across = jax.random.randint(jax.random.fold_in(key, 2), (2, LEV, NLAT, NLON), -HMAX, HMAX)
    return jnp.concatenate([vertical, across], axis=0).astype(jnp.int32)


def draw_depart_first(key, part):
    return offsets_first(jax.random.fold_in(key, 11))


def draw_depart_second(key, part):
    first = offsets_first(jax.random.fold_in(key, 11))
    extra = jax.random.randint(jax.random.fold_in(key, 12), first.shape, 0, 2)
    return jnp.floor_divide(first + extra, 2).astype(jnp.int32)


def draw_winds(key, part):
    first = offsets_first(jax.random.fold_in(key, 11)).astype(jnp.float32)
    phase = jax.random.uniform(jax.random.fold_in(key, 13), first.shape, jnp.float32, -0.25, 1.25)
    return -(first + phase)


def touch_ends(entries, stream_key, low, top_value):
    longest = entries.shape.index(max(entries.shape))
    spots = []
    for shift in (0, 1):
        where = [jax.random.randint(jax.random.fold_in(stream_key, axis), (), 0, length) for axis, length in enumerate(entries.shape)]
        where[longest] = (where[longest] + shift) % entries.shape[longest]
        spots.append(tuple(where))
    return entries.at[spots[0]].set(low).at[spots[1]].set(top_value)


def level_of(rng, extent, pieces, smallest, largest):
    gain, own = 1.0, jax.random.fold_in(rng, 6)
    for dim, blocks in pieces:
        steps = jnp.exp(jax.random.uniform(jax.random.fold_in(own, dim), (blocks,), jnp.float32, smallest / len(pieces), largest / len(pieces)))
        gain = gain * jnp.repeat(steps, extent[dim] // blocks).reshape([-1 if axis == dim else 1 for axis in range(len(extent))])
    return gain


def deal_out(key, own, number, rows, count, top, reach, lean):
    order = jax.random.permutation(key, count)
    crowded, usual = load_shares(count, rows * top, reach, lean, True), load_shares(count, rows * top, reach, lean, False)
    places = jnp.arange(count)

    def named(tallies, offset_by):
        used = int((tallies > 0).sum())
        fixed = max(1, used // 4)
        passed = fixed + (places - fixed + offset_by * (used - fixed)) % max(1, count - fixed)
        return jnp.zeros((count,), jnp.int32).at[order[jnp.where(places < fixed, places, passed)]].set(jnp.asarray(tallies, jnp.int32))

    tallies = jnp.where(number % 4 == 0, named(crowded, number // 4), named(usual, number - number // 4 - 1))
    mixed = jax.random.permutation(jax.random.fold_in(own, 3), count)
    source_of, sink = mixed[0:count // 2 * 2:2], mixed[1:count // 2 * 2:2]
    slack = jnp.minimum(tallies[source_of] - 1, reach - tallies[sink]) // 2
    slack = jnp.where((source_of == order[0]) | (sink == order[0]) | (tallies[sink] == 0), 0, jnp.maximum(slack, 0))
    passed = jax.random.randint(jax.random.fold_in(own, 4), (count // 2,), 0, 1 << 20) % (slack + 1)
    tallies = tallies.at[source_of].add(-passed).at[sink].add(passed)
    labels = jnp.searchsorted(jnp.cumsum(tallies), jnp.arange(rows * top), side="right").astype(jnp.int32)
    table = labels.reshape(top, rows).T
    table = table[jax.random.permutation(jax.random.fold_in(own, 1), rows)]
    offset_by = jax.random.randint(jax.random.fold_in(own, 2), (rows, 1), 0, top)
    return jnp.take_along_axis(table, (jnp.arange(top)[None, :] + offset_by) % top, axis=1)


def load_shares(amount, total, most, slope, full):
    loads = [(1 << 20) // math.isqrt(grade ** slope) + 1 for grade in range(1, amount + 1)]
    largest = most if full else min(most, max(-(-total // amount), total * loads[0] // sum(loads)))
    least = 1 if total - largest >= amount - 1 else 0
    counts, surplus = [largest] + [least] * (amount - 1), total - largest - least * (amount - 1)
    while surplus > 0:
        movable = [i for i in range(1, amount) if counts[i] < largest] or [i for i in range(1, amount) if counts[i] < most]
        pool, left = sum([loads[i] for i in movable]), surplus
        for i in movable:
            addition = min(most - counts[i], max(1, left * loads[i] // pool), surplus)
            counts[i] = counts[i] + addition
            surplus = surplus - addition
    return np.array(counts)


def bell_draw(key, dims, deviation, bound, cuts=(), held_as=jnp.bfloat16):
    result = deviation * jax.random.normal(key, dims, jnp.float32)
    if cuts:
        result = result * level_of(key, dims, cuts, -0.22, 0.18)
    return jnp.clip(result, -bound, bound).astype(held_as)


def setup_inputs(seed: int = 0) -> dict:
    key_of = jax.random.split(jax.random.key(seed), 9)
    tracers = bell_draw(key_of[0], (NTR, LEV, NLAT, NLON), 1.0, 6.0, ((2, 4), (3, 8)), jnp.float32)
    winds = draw_winds(jax.random.fold_in(key_of[8], 71), 0)
    depart_first = draw_depart_first(jax.random.fold_in(key_of[8], 71), 0)
    depart_second = draw_depart_second(jax.random.fold_in(key_of[8], 71), 0)
    fluxes = jnp.clip(jnp.exp(math.log(5.0) - 4.609084 * jax.random.uniform(key_of[4], (TILES, ROWS, TILE_CELLS), jnp.float32) ** level_of(key_of[4], (TILES, ROWS, TILE_CELLS), ((0, 32),), -0.2, 0.2)), 0.049804688, 5.0).astype(jnp.bfloat16)
    remap_weights = jnp.clip(jnp.exp(math.log(0.019897461) - 4.603446 * jax.random.uniform(key_of[5], (TILES, K, TILE_CELLS, BCOLS), jnp.float32) ** level_of(key_of[5], (TILES, K, TILE_CELLS, BCOLS), ((0, 32),), -0.2, 0.2)), 0.00019931793, 0.019897461).astype(jnp.bfloat16)
    target_device_keys = jax.random.split(jax.random.fold_in(key_of[6], 1), TILES // NTILE)
    target_device_turns = jax.random.permutation(jax.random.fold_in(key_of[6], 3), TILES // NTILE)
    target_device = jax.vmap(lambda own, number: deal_out(jax.random.fold_in(key_of[6], 2), own, number, NTILE, DEVICES, K, CAP, 2))(target_device_keys, target_device_turns).reshape((TILES, K))
    target_block = touch_ends(jax.random.randint(key_of[7], (TILES, K), 0, BLK_DEV), jax.random.fold_in(key_of[7], 1), 0, BLK_DEV - 1).astype(jnp.int32)
    return {"tracers": tracers, "winds": winds, "depart_first": depart_first, "depart_second": depart_second, "fluxes": fluxes, "remap_weights": remap_weights, "target_device": target_device, "target_block": target_block}


def cubic_weights(frac):
    first = -frac * (frac - 1.0) * (frac - 2.0) / 6.0
    second = (frac + 1.0) * (frac - 1.0) * (frac - 2.0) / 2.0
    third = -(frac + 1.0) * frac * (frac - 2.0) / 2.0
    fourth = (frac + 1.0) * frac * (frac - 1.0) / 6.0
    return (first, second, third, fourth)


def tricubic(padded, base, frac):
    chans, levels, rows, cols = padded.shape
    flat = padded.reshape(chans, levels * rows * cols)
    level_w = cubic_weights(frac[0])
    row_w = cubic_weights(frac[1])
    col_w = jnp.stack(cubic_weights(frac[2]))
    col_index = jnp.stack([base[2] + step for step in (-1, 0, 1, 2)]).astype(jnp.int32)
    total = jnp.zeros((chans,) + base.shape[1:], jnp.float32)
    for above in range(4):
        level_index = jnp.clip(base[0] + above - 1, 0, levels - 1).astype(jnp.int32)
        for across in range(4):
            row_index = (base[1] + across - 1).astype(jnp.int32)
            index = ((level_index * rows + row_index) * cols)[None] + col_index
            picked = jnp.take(flat, index.reshape(-1), axis=1).reshape((chans,) + index.shape)
            summed = jnp.sum(picked * col_w[None], axis=1)
            total = total + (level_w[above] * row_w[across])[None] * summed
    return total


def per_channel(padded, base, frac):
    return lax.map(lambda single: tricubic(single[None], base, frac)[0], padded)


def extend(field, width):
    padded = jnp.pad(field, ((0, 0), (0, 0), (width, width), (0, 0)))
    return jnp.concatenate([padded[..., -width:], padded, padded[..., :width]], axis=3)


def reference(tracers, winds, depart_first, depart_second, fluxes, remap_weights, target_device, target_block):
    width = HMAX + 1
    shape = (LEV, NLAT, NLON)
    position = jnp.stack([
        lax.broadcasted_iota(jnp.int32, shape, 0),
        lax.broadcasted_iota(jnp.int32, shape, 1) + width,
        lax.broadcasted_iota(jnp.int32, shape, 2) + width,
    ])
    frac_first = jnp.clip(-winds - depart_first.astype(winds.dtype), 0.0, 1.0)
    midwind = per_channel(extend(winds, width), position + depart_first, frac_first)
    frac_second = jnp.clip(-(winds + midwind) * 0.5 - depart_second.astype(winds.dtype), 0.0, 1.0)
    moved = per_channel(extend(tracers, width), position + depart_second, frac_second)

    groups = TILES // NTILE
    block_ids = (target_device * BLK_DEV + target_block).astype(jnp.int32)

    def accumulate(total, piece):
        flux_group, weight_group, id_group = piece
        product = jnp.einsum("trc,tkcb->tkrb", flux_group.astype(jnp.float32), weight_group.astype(jnp.float32))
        product = lax.optimization_barrier(product.astype(jnp.bfloat16)).astype(jnp.float32)
        total = total.at[id_group.reshape(-1)].add(product.reshape(-1, ROWS, BCOLS))
        return total, None

    start = jnp.zeros((groups * BLK_DEV, ROWS, BCOLS), jnp.float32)
    blocks, unused = lax.scan(accumulate, start, (
        fluxes.reshape(groups, NTILE, ROWS, TILE_CELLS),
        remap_weights.reshape(groups, NTILE, K, TILE_CELLS, BCOLS),
        block_ids.reshape(groups, NTILE, K)))
    grid = blocks.reshape(N_LAT, N_LON, BLK_DEV, NTR, LEV, BCOLS).transpose(3, 4, 0, 1, 2, 5)
    grid = grid.reshape(NTR, LEV, N_LAT, N_LON, CLAT, CLON).transpose(0, 1, 2, 4, 3, 5)
    emission = grid.reshape(NTR, LEV, NLAT, NLON)
    return moved + emission
```

```python
import functools

import jax
import jax.numpy as jnp
from jax import lax
from jax.experimental import pallas as pl
from jax.experimental.pallas import tpu as pltpu
from jax.sharding import PartitionSpec as P

NTR = 16
CAP = 2
BLK_DEV = 16
HMAX = 3


def padded_2(block, sides, width, periodic):
    for axis, dim in sides:
        count = lax.axis_size(axis)
        forward = [(i, i + 1) for i in range(count - 1)]
        if periodic:
            forward.append((count - 1, 0))
        backward = [(target, source) for source, target in forward]
        low = lax.ppermute(
            lax.slice_in_dim(block, block.shape[dim] - width, None, axis=dim), axis, forward
        )
        high = lax.ppermute(lax.slice_in_dim(block, 0, width, axis=dim), axis, backward)
        block = jnp.concatenate([low, block, high], axis=dim)
    return block


def cubic_weights(frac):
    first = -frac * (frac - 1.0) * (frac - 2.0) / 6.0
    second = (frac + 1.0) * (frac - 1.0) * (frac - 2.0) / 2.0
    third = -(frac + 1.0) * frac * (frac - 2.0) / 2.0
    fourth = (frac + 1.0) * frac * (frac - 1.0) / 6.0
    return (first, second, third, fourth)


def level_weights(offset, frac):
    s0, s1, s2, s3 = cubic_weights(frac)
    down = offset < 0
    zero = jnp.zeros_like(frac)
    return [
        jnp.where(down, s0, zero),
        jnp.where(down, s1, s0),
        jnp.where(down, s2, s1),
        jnp.where(down, s3, s2),
        jnp.where(down, zero, s3),
    ]


def offset_weights(offset, frac, reach):
    stencil = cubic_weights(frac)
    spread = []
    for target in range(-reach, reach + 1):
        weight = jnp.zeros(frac.shape, jnp.float32)
        for step in range(4):
            weight = jnp.where(offset == target - step + 1, stencil[step], weight)
        spread.append(weight)
    return spread


def advect_kernel(
    wide, narrow, winds_ref, first_ref, second_ref, wpad_ref, main_ref, halo_ref, out_ref,
    shifted, lhs, rhs, mid_ref, lev_w, row_w, col_w, col_at
):
    levels, height, chans, lanes = main_ref.shape
    comps, rows = winds_ref.shape[0], winds_ref.shape[1]
    taps, reach = 2 * wide + 1, 2 * narrow + 1

    def shift_row(r, carry):
        for comp in range(comps):
            row = wpad_ref[comp, r]
            for e in range(taps):
                piece = row[:, e : e + lanes]
                low, high = piece[:1], piece[levels - 1 :]
                shifted[e * 5 + 0, comp, r] = jnp.concatenate([low, low, piece[: levels - 2]], axis=0)
                shifted[e * 5 + 1, comp, r] = jnp.concatenate([low, piece[: levels - 1]], axis=0)
                shifted[e * 5 + 2, comp, r] = piece
                shifted[e * 5 + 3, comp, r] = jnp.concatenate([piece[1:], high], axis=0)
                shifted[e * 5 + 4, comp, r] = jnp.concatenate([piece[2:], high, high], axis=0)
        return carry

    lax.fori_loop(0, wpad_ref.shape[1], shift_row, 0)

    def wind_row(i, carry):
        wind = [winds_ref[comp, i] for comp in range(comps)]
        off = [first_ref[comp, i] for comp in range(comps)]
        frac = [
            jnp.clip(-wind[comp] - off[comp].astype(jnp.float32), 0.0, 1.0) for comp in range(comps)
        ]
        lw = level_weights(off[0], frac[0])
        rw = offset_weights(off[1], frac[1], wide)
        cw = offset_weights(off[2], frac[2], wide)
        total = [jnp.zeros((levels, lanes), jnp.float32) for comp in range(comps)]
        for across in range(taps):
            for above in range(5):
                pair = lw[above] * rw[across]
                for comp in range(comps):
                    inner = cw[0] * shifted[above, comp, i + across]
                    for e in range(1, taps):
                        inner = inner + cw[e] * shifted[e * 5 + above, comp, i + across]
                    total[comp] = total[comp] + pair * inner
        off = [second_ref[comp, i] for comp in range(comps)]
        frac = [
            jnp.clip(
                -(wind[comp] + total[comp]) * 0.5 - off[comp].astype(jnp.float32), 0.0, 1.0
            )
            for comp in range(comps)
        ]
        for n, weight in enumerate(level_weights(off[0], frac[0])):
            lev_w[n, i] = weight
        for n, weight in enumerate(offset_weights(off[1], frac[1], narrow)):
            row_w[n, i] = weight
        for n, weight in enumerate(cubic_weights(frac[2])):
            col_w[n, i] = weight
        col_at[i] = off[2] - 1 + lax.broadcasted_iota(jnp.int32, (levels, lanes), 1)
        return carry

    lax.fori_loop(0, rows, wind_row, 0)

    lane = lax.broadcasted_iota(jnp.int32, (chans, lanes), 1)
    is_low = jnp.logical_and(lane >= 8, lane < 16)

    def split_row(r, carry):
        for level in range(levels + 4):
            at = min(max(level - 2, 0), levels - 1)
            value = main_ref[at, r]
            top = value.astype(jnp.bfloat16)
            rest = (value - top.astype(jnp.float32)).astype(jnp.bfloat16)
            edge = halo_ref[at, r]
            edge_top = edge.astype(jnp.bfloat16).astype(jnp.float32)
            edge = jnp.where(is_low, edge - edge_top, edge_top).astype(jnp.bfloat16)
            lhs[level, r, :, 0:lanes] = top
            lhs[level, r, :, lanes : 2 * lanes] = rest
            lhs[level, r, :, 2 * lanes : 3 * lanes] = top
            lhs[level, r, :, 3 * lanes : 4 * lanes] = edge
        return carry

    lax.fori_loop(0, height, split_row, 0)

    rhs[...] = jnp.zeros_like(rhs)
    inside = lax.broadcasted_iota(jnp.int32, (lanes, lanes), 0)
    spot = lax.broadcasted_iota(jnp.int32, (8, lanes), 0)
    outside = jnp.where(spot < 4, spot - 4, spot + (lanes - 4))

    def step(t, carry):
        level, first_row = t // (rows // 2), (t % (rows // 2)) * 2
        for side in range(2):
            i = first_row + side
            at = col_at[i, pl.ds(level, 1), :]
            weights = [col_w[n, i, pl.ds(level, 1), :] for n in range(4)]
            cols = slice(side * lanes, (side + 1) * lanes)

            def spread(where):
                away = where - at
                value = jnp.where(away == 0, weights[0], 0.0)
                for n in range(1, 4):
                    value = jnp.where(away == n, weights[n], value)
                top = value.astype(jnp.bfloat16).astype(jnp.float32)
                return top, value - top

            top, rest = spread(inside)
            top16 = top.astype(jnp.bfloat16)
            rhs[0:lanes, cols] = top16
            rhs[lanes : 2 * lanes, cols] = top16
            rhs[2 * lanes : 3 * lanes, cols] = rest.astype(jnp.bfloat16)
            top, rest = spread(outside)
            rhs[3 * lanes : 3 * lanes + 32, cols] = jnp.concatenate(
                [top, top, rest, jnp.zeros_like(rest)], axis=0
            ).astype(jnp.bfloat16)
        span = reach + 1
        left = lhs[pl.ds(level, 5), pl.ds(first_row, span)].reshape(5 * span * chans, 4 * lanes)
        done = jnp.dot(left, rhs[...], preferred_element_type=jnp.float32)
        for side in range(2):
            i = first_row + side
            cols = slice(side * lanes, (side + 1) * lanes)
            rw = [row_w[n, i, pl.ds(level, 1), :] for n in range(reach)]
            total = jnp.zeros((chans, lanes), jnp.float32)
            for above in range(5):
                lw = lev_w[above, i, pl.ds(level, 1), :]
                inner = jnp.zeros((chans, lanes), jnp.float32)
                for n in range(reach):
                    start = (above * span + n + side) * chans
                    inner = inner + rw[n] * done[start : start + chans, cols]
                total = total + lw * inner
            out_ref[level, i] = total
        return carry

    lax.fori_loop(0, levels * (rows // 2), step, 0)


def advect(winds, depart_first, depart_second, wind_wide, tracer_wide, wide, narrow):
    chans, levels, height, _ = tracer_wide.shape
    comps, _, rows, lanes = winds.shape
    by_row = lambda array: array.transpose(0, 2, 1, 3)
    turned = tracer_wide.transpose(1, 2, 0, 3)
    main = turned[..., narrow : narrow + lanes]
    edge = jnp.concatenate([turned[..., :narrow], turned[..., narrow + lanes :]], axis=3)
    gap = jnp.zeros(edge.shape[:3] + (4 - narrow,), jnp.float32)
    edge = jnp.concatenate([gap, edge, gap], axis=3)
    halo = jnp.concatenate(
        [edge, edge, edge, jnp.zeros(edge.shape[:3] + (lanes - 24,), jnp.float32)], axis=3
    )
    vmem = pl.BlockSpec(memory_space=pltpu.VMEM)
    moved = pl.pallas_call(
        functools.partial(advect_kernel, wide, narrow),
        out_shape=jax.ShapeDtypeStruct((levels, rows, chans, lanes), jnp.float32),
        in_specs=[vmem] * 6,
        out_specs=vmem,
        scratch_shapes=[
            pltpu.VMEM((5 * (2 * wide + 1), comps, rows + 2 * wide, levels, lanes), jnp.float32),
            pltpu.VMEM((levels + 4, height, chans, 4 * lanes), jnp.bfloat16),
            pltpu.VMEM((4 * lanes, 2 * lanes), jnp.bfloat16),
            pltpu.VMEM((comps, rows, levels, lanes), jnp.float32),
            pltpu.VMEM((5, rows, levels, lanes), jnp.float32),
            pltpu.VMEM((2 * narrow + 1, rows, levels, lanes), jnp.float32),
            pltpu.VMEM((4, rows, levels, lanes), jnp.float32),
            pltpu.VMEM((rows, levels, lanes), jnp.int32),
        ],
        compiler_params=pltpu.CompilerParams(vmem_limit_bytes=48 * 1024 * 1024),
        cost_estimate=pl.CostEstimate(flops=10**10, bytes_accessed=10**7, transcendentals=0),
        name="advect",
    )(by_row(winds), by_row(depart_first), by_row(depart_second), by_row(wind_wide), main, halo)
    return moved.transpose(2, 0, 1, 3)


def body(
    tracers, winds, depart_first, depart_second, fluxes, remap_weights, target_device, target_block
):
    wide = HMAX + 1
    narrow = max((HMAX + 1) // 2 + 1, HMAX // 2 + 2)
    wind_side = padded_2(winds, (("lon", 3),), wide, True)
    wind_wide = padded_2(wind_side, (("lat", 2),), wide, False)
    tracer_side = padded_2(tracers, (("lon", 3),), narrow, True)
    tracer_wide = padded_2(tracer_side, (("lat", 2),), narrow, False)
    shape = winds.shape[1:]
    moved = advect(winds, depart_first, depart_second, wind_wide, tracer_wide, wide, narrow)
    tiles, links = target_device.shape
    rows_count, block_cols = (fluxes.shape[1], remap_weights.shape[3])
    items = tiles * links
    remapped = jnp.einsum(
        "trc,tkcb->tkrb", fluxes, remap_weights, preferred_element_type=jnp.float32
    )
    remapped = remapped.astype(jnp.bfloat16).reshape(items, rows_count, block_cols)
    lat_count = lax.axis_size("lat")
    lon_count = lax.axis_size("lon")
    devices = lat_count * lon_count
    slot_count = devices * CAP
    owners = target_device.reshape(items)
    item_iota = lax.broadcasted_iota(jnp.int32, (items, items), 1)
    item_rows = lax.broadcasted_iota(jnp.int32, (items, items), 0)
    earlier = jnp.logical_and(owners[:, None] == owners[None, :], item_iota < item_rows)
    rank = jnp.sum(earlier.astype(jnp.int32), axis=1)
    slot = owners * CAP + rank
    slot_iota = lax.broadcasted_iota(jnp.int32, (slot_count, items), 0)
    hit = slot[None, :] == slot_iota
    present = jnp.any(hit, axis=1)
    source_item = jnp.sum(
        jnp.where(hit, lax.broadcasted_iota(jnp.int32, (slot_count, items), 1), 0), axis=1
    )
    outgoing = jnp.take(remapped, source_item, axis=0)
    outgoing = jnp.where(present[:, None, None], outgoing, jnp.zeros_like(outgoing))
    labels = jnp.where(present, jnp.take(target_block.reshape(items), source_item), -1)
    data = outgoing.reshape(devices, CAP, rows_count, block_cols)
    marks = labels.reshape(devices, CAP)
    arrived, arrived_labels = (
        lax.all_to_all(data, ("lat", "lon"), split_axis=0, concat_axis=0, tiled=True),
        lax.all_to_all(marks, ("lat", "lon"), split_axis=0, concat_axis=0, tiled=True),
    )
    arrived_flat = arrived.reshape(slot_count, rows_count * block_cols)
    block_iota = lax.broadcasted_iota(jnp.int32, (BLK_DEV, slot_count), 0)
    selector = (arrived_labels.reshape(1, slot_count) == block_iota).astype(jnp.bfloat16)
    blocks = jnp.dot(selector, arrived_flat, preferred_element_type=jnp.float32)
    levels, lat_rows, lon_cols = shape
    grid = blocks.reshape(BLK_DEV, NTR, levels, block_cols).transpose(1, 2, 0, 3)
    return moved + grid


def solution(mesh):
    in_specs = (
        P(None, None, "lat", "lon"),
        P(None, None, "lat", "lon"),
        P(None, None, "lat", "lon"),
        P(None, None, "lat", "lon"),
        P(("lat", "lon"), None, None),
        P(("lat", "lon"), None, None, None),
        P(("lat", "lon"), None),
        P(("lat", "lon"), None),
    )
    out_specs = P(None, None, "lat", "lon")
    return jax.shard_map(body, mesh=mesh, in_specs=in_specs, out_specs=out_specs, check_vma=False)
```
